32 devices in a mesh: blk: 16 (over z, x, core), ep: 2 (over y).
Axes of the slice: x: 2, y: 2, z: 4, core: 2. Of those that a mesh axis runs over, the one named last changes fastest.
Arguments:
- hidden_in: bfloat16 [256, 4096], P('blk'), may hold values from -6 to 6
- out_grad: bfloat16 [256, 4096], P('blk'), may hold values from -6 to 6
- expert_ids: int32 [256, 2], P('blk'), may hold values from 0 to 3, all different within a row; in each aligned block of 16 rows (0 to 15, 16 to 31, ...) at most 12 rows name the same one
- gate_values: bfloat16 [256, 2], P('blk'), may hold values from 0.099609375 to 1
- w_gate: bfloat16 [4, 14336, 4096], P('ep', 'blk'), may hold values from -0.09375 to 0.09375
- w_up: bfloat16 [4, 14336, 4096], P('ep', 'blk'), may hold values from -0.09375 to 0.09375
- w_down: bfloat16 [4, 14336, 4096], P('ep', 'blk'), may hold values from -0.046875 to 0.046875
Outputs:
- input_grad: bfloat16 [256, 4096], P('blk')
- gate_grad: float32 [256, 2], P('blk')
- grad_gate: bfloat16 [4, 14336, 4096], P('ep', 'blk')
- grad_up: bfloat16 [4, 14336, 4096], P('ep', 'blk')
- grad_down: bfloat16 [4, 14336, 4096], P('ep', 'blk')
The draws below stay inside these ranges and needn't reach their ends.
Inputs may be any that keep to these rules, and one draw needn't show every extreme that they name: `expert_ids`: each row names 2 different experts; in each aligned block of 16 rows (the rows of one device) no expert is named by more than 12 rows, a bound that some block reaches.
All inputs are finite; a program needn't handle non-finite values.
Results may differ from the reference program's by a relative error of at most 0.008.
Values may be sent and summed in bfloat16 or wider, within the bound.
A program may use at most 256 MiB of HBM per device.

```python
import math
import jax
import jax.numpy as jnp
import numpy as np
from jax import lax

D = 4096
FF = 14336
TOP = 2
TOK_DEV = 16
EXPERTS = 4
CAP = 12
TOKENS = 256


def block_scale(own_key, shape, split, low, largest):
    loudness, own = 1.0, jax.random.fold_in(own_key, 6)
    for dim, blocks in split:
        steps = jnp.exp(jax.random.uniform(jax.random.fold_in(own, dim), (blocks,), jnp.float32, low / len(split), largest / len(split)))
        loudness = loudness * jnp.repeat(steps, shape[dim] // blocks).reshape([-1 if axis == dim else 1 for axis in range(len(shape))])
    return loudness


def shared_out(rng, own, number, rows, count, top, most, lean):
    sequence = jax.random.permutation(rng, count)
    crowded, usual = portions_of(count, rows * top, most, lean, True), portions_of(count, rows * top, most, lean, False)
    places = jnp.arange(count)

    def named(lengths, offset_by):
        used = int((lengths > 0).sum())
        fixed = max(1, used // 4)
        passed = fixed + (places - fixed + offset_by * (used - fixed)) % max(1, count - fixed)
        return jnp.zeros((count,), jnp.int32).at[sequence[jnp.where(places < fixed, places, passed)]].set(jnp.asarray(lengths, jnp.int32))

    lengths = jnp.where(number % 4 == 0, named(crowded, number // 4), named(usual, number - number // 4 - 1))
    mixed = jax.random.permutation(jax.random.fold_in(own, 3), count)
    giver, sink = mixed[0:count // 2 * 2:2], mixed[1:count // 2 * 2:2]
    margin = jnp.minimum(lengths[giver] - 1, most - lengths[sink]) // 2
    margin = jnp.where((giver == sequence[0]) | (sink == sequence[0]) | (lengths[sink] == 0), 0, jnp.maximum(margin, 0))
    passed = jax.random.randint(jax.random.fold_in(own, 4), (count // 2,), 0, 1 << 20) % (margin + 1)
    lengths = lengths.at[giver].add(-passed).at[sink].add(passed)
    items = jnp.searchsorted(jnp.cumsum(lengths), jnp.arange(rows * top), side="right").astype(jnp.int32)
    table = items.reshape(top, rows).T
    table = table[jax.random.permutation(jax.random.fold_in(own, 1), rows)]
    offset_by = jax.random.randint(jax.random.fold_in(own, 2), (rows, 1), 0, top)
    return jnp.take_along_axis(table, (jnp.arange(top)[None, :] + offset_by) % top, axis=1)


def portions_of(number_of, total, bound, slope, full):
    loads = [(1 << 20) // math.isqrt(standing ** slope) + 1 for standing in range(1, number_of + 1)]
    largest = bound if full else min(bound, max(-(-total // number_of), total * loads[0] // sum(loads)))
    least = 1 if total - largest >= number_of - 1 else 0
    given, spare = [largest] + [least] * (number_of - 1), total - largest - least * (number_of - 1)
    while spare > 0:
        free = [i for i in range(1, number_of) if given[i] < largest] or [i for i in range(1, number_of) if given[i] < bound]
        mass, left = sum([loads[i] for i in free]), spare
        for i in free:
            addition = min(bound - given[i], max(1, left * loads[i] // mass), spare)
            given[i] = given[i] + addition
            spare = spare - addition
    return np.array(given)


def scatter_about(rng, extent, scale, bound, cuts=(), held_as=jnp.bfloat16):
    values = jax.random.normal(rng, extent, jnp.float32) * scale
    if len(cuts) > 0:
        values = block_scale(rng, extent, cuts, -0.22, 0.18) * values
    return jnp.clip(values, min=-bound, max=bound).astype(held_as)


def setup_inputs(seed: int = 0) -> dict:
    splits = jax.random.split(jax.random.key(seed), 8)
    hidden_in = scatter_about(splits[0], (TOKENS, D), 1.0, 6.0, ((0, 16),))
    out_grad = scatter_about(splits[1], (TOKENS, D), 1.0, 6.0, ((0, 16),))
    expert_ids_keys = jax.random.split(jax.random.fold_in(splits[2], 1), TOKENS // TOK_DEV)
    expert_ids_turns = jax.random.permutation(jax.random.fold_in(splits[2], 3), TOKENS // TOK_DEV)
    expert_ids = jax.vmap(lambda own, number: shared_out(jax.random.fold_in(splits[2], 2), own, number, TOK_DEV, EXPERTS, TOP, CAP, 2))(expert_ids_keys, expert_ids_turns).reshape((TOKENS, TOP))
    gate_values = jnp.clip(jnp.exp(math.log(1.0) - 2.306499 * jax.random.uniform(splits[3], (TOKENS, TOP), jnp.float32) ** block_scale(splits[3], (TOKENS, TOP), ((0, 16),), -0.2, 0.2)), 0.099609375, 1.0).astype(jnp.bfloat16)
    w_gate = scatter_about(splits[4], (EXPERTS, FF, D), D ** -0.5, 0.09375, ((0, 2), (1, 16)))
    w_up = scatter_about(splits[5], (EXPERTS, FF, D), D ** -0.5, 0.09375, ((0, 2), (1, 16)))
    w_down = scatter_about(splits[6], (EXPERTS, FF, D), FF ** -0.5, 0.046875, ((0, 2), (1, 16)))
    return dict(hidden_in=hidden_in, out_grad=out_grad, expert_ids=expert_ids, gate_values=gate_values, w_gate=w_gate, w_up=w_up, w_down=w_down)


def routed(expert_ids, gate_values, expert, blocks):
    chosen = expert_ids == expert
    hits = jnp.any(chosen, axis=1).astype(jnp.int32).reshape(blocks, TOK_DEV)
    weight = jnp.sum(jnp.where(chosen, gate_values.astype(jnp.float32), jnp.float32(0.0)), axis=1).reshape(blocks, TOK_DEV)
    position = jnp.cumsum(hits, axis=1) - hits
    slot_index = lax.broadcasted_iota(jnp.int32, (blocks, CAP, TOK_DEV), 1)
    picked = (position[:, None, :] == slot_index) & (hits[:, None, :] > 0)
    selector = jnp.where(picked, jnp.float32(1.0), jnp.float32(0.0))
    return selector, weight, chosen


def expert_pass(selector, weight, hidden_in, out_grad, gate_mat, up_mat, down_mat, blocks):
    width = hidden_in.shape[1]
    high = lax.Precision.HIGHEST
    x_slots = jnp.einsum("bct,btd->bcd", selector, hidden_in.reshape(blocks, TOK_DEV, width).astype(jnp.float32), precision=high).astype(jnp.bfloat16).reshape(-1, width)
    dy_slots = jnp.einsum("bct,btd->bcd", selector, out_grad.reshape(blocks, TOK_DEV, width).astype(jnp.float32), precision=high).astype(jnp.bfloat16).reshape(-1, width)
    slot_weight = jnp.einsum("bct,bt->bc", selector, weight, precision=high).reshape(-1, 1)
    gate_pre = jnp.dot(x_slots, gate_mat.T, preferred_element_type=jnp.float32)
    up_pre = jnp.dot(x_slots, up_mat.T, preferred_element_type=jnp.float32)
    back = jnp.dot(dy_slots, down_mat.T, preferred_element_type=jnp.float32)
    sigmoid_gate = jax.nn.sigmoid(gate_pre)
    activation = gate_pre * sigmoid_gate * up_pre
    slot_gate = jnp.sum(activation * back, axis=1)
    dact = slot_weight * back
    d_up = (dact * gate_pre * sigmoid_gate).astype(jnp.bfloat16)
    d_gate = (dact * up_pre * sigmoid_gate * (1.0 + gate_pre * (1.0 - sigmoid_gate))).astype(jnp.bfloat16)
    act_low = activation.astype(jnp.bfloat16)
    dy_weighted = (slot_weight * dy_slots.astype(jnp.float32)).astype(jnp.bfloat16)
    grad_g = jnp.dot(d_gate.T, x_slots, preferred_element_type=jnp.float32).astype(jnp.bfloat16)
    grad_u = jnp.dot(d_up.T, x_slots, preferred_element_type=jnp.float32).astype(jnp.bfloat16)
    grad_d = jnp.dot(act_low.T, dy_weighted, preferred_element_type=jnp.float32).astype(jnp.bfloat16)
    dx_slots = jnp.dot(d_gate, gate_mat, preferred_element_type=jnp.float32) + jnp.dot(d_up, up_mat, preferred_element_type=jnp.float32)
    dx_tokens = jnp.einsum("bct,bcd->btd", selector, dx_slots.reshape(blocks, CAP, width), precision=high).reshape(-1, width)
    gate_tokens = jnp.einsum("bct,bc->bt", selector, slot_gate.reshape(blocks, CAP), precision=high).reshape(-1)
    return grad_g, grad_u, grad_d, dx_tokens, gate_tokens


def reference(hidden_in, out_grad, expert_ids, gate_values, w_gate, w_up, w_down):
    blocks = hidden_in.shape[0] // TOK_DEV
    token_grad = jnp.zeros(hidden_in.shape, jnp.float32)
    gate_grad = jnp.zeros(expert_ids.shape, jnp.float32)
    grads_g, grads_u, grads_d = [], [], []
    for expert in range(w_gate.shape[0]):
        selector, weight, chosen = routed(expert_ids, gate_values, expert, blocks)
        grad_g, grad_u, grad_d, dx_tokens, gate_tokens = expert_pass(selector, weight, hidden_in, out_grad, w_gate[expert], w_up[expert], w_down[expert], blocks)
        grads_g.append(grad_g)
        grads_u.append(grad_u)
        grads_d.append(grad_d)
        token_grad = token_grad + dx_tokens
        gate_grad = gate_grad + jnp.where(chosen, gate_tokens[:, None], jnp.float32(0.0))
    return (token_grad.astype(jnp.bfloat16), gate_grad, jnp.stack(grads_g), jnp.stack(grads_u), jnp.stack(grads_d))
```

```python
import functools

import jax
import jax.numpy as jnp
from jax import lax
from jax.experimental import pallas as pl
from jax.experimental.pallas import tpu as pltpu
from jax.sharding import PartitionSpec as P

MESH = pl.DeviceIdType.MESH
CHUNKS = 4
VMEM_LIMIT = 62 * 1024 * 1024


def greet(blk_peers, ep_peers):
    barrier = pltpu.get_barrier_semaphore()
    for peer in blk_peers:
        pl.semaphore_signal(barrier, inc=1, device_id={"blk": peer}, device_id_type=MESH)
    for peer in ep_peers:
        pl.semaphore_signal(barrier, inc=1, device_id={"ep": peer}, device_id_type=MESH)
    pl.semaphore_wait(barrier, len(blk_peers) + len(ep_peers))


def forward_kernel(
    n, x_in, dy_in, w_in, w_gate, w_up, w_down,
    x_all, dy_all, dg_t, du_t, aw_t, sg,
    w_all, wbuf, acc, wsem, own_sem, send_sem, recv_sem, fsend_sem, frecv_sem,
    wsend_sem, wrecv_sem, wfsend_sem, wfrecv_sem,
):
    experts, hidden, width = w_gate.shape
    tb, tokens = x_in.shape[0], x_all.shape[0]
    chunks, half = CHUNKS, n // 2
    dc = width // chunks
    mats = (w_gate, w_up, w_down)
    kinds = ((x_in, x_all), (dy_in, dy_all))
    me = lax.axis_index("blk")
    partner = me + 1 - 2 * lax.rem(me, 2)

    def cols(c):
        return pl.ds(pl.multiple_of(c * dc, dc), dc)

    def rows(o):
        return pl.ds(pl.multiple_of(o * tb, tb), tb)

    def tile(c, e, m):
        slot = e * 3 + m
        return pltpu.make_async_copy(mats[m].at[e, :, cols(c)], wbuf.at[slot], wsem.at[slot])

    for e in range(experts):
        for m in range(3):
            tile(0, e, m).start()
    own = [
        pltpu.make_async_copy(x_in, x_all.at[rows(me)], own_sem.at[0]),
        pltpu.make_async_copy(dy_in, dy_all.at[rows(me)], own_sem.at[1]),
        pltpu.make_async_copy(w_in, w_all.at[me], own_sem.at[2]),
    ]
    for copy in own:
        copy.start()

    greet([partner] + [lax.rem(me + 2 * k, n) for k in range(1, half)], [])

    def remote(src, dst, ssem, rsem, to):
        return pltpu.make_async_remote_copy(
            src_ref=src, dst_ref=dst, send_sem=ssem, recv_sem=rsem,
            device_id={"blk": to}, device_id_type=MESH,
        )

    def send(i, c, k):
        src, dst = kinds[i]
        return remote(
            src.at[:, cols(c)], dst.at[rows(me), cols(c)],
            send_sem.at[i, c, k], recv_sem.at[i, c, k], lax.rem(me + 2 * k, n),
        )

    def arrive(i, c, k):
        dst = kinds[i][1].at[rows(lax.rem(me + n - 2 * k, n)), cols(c)]
        return remote(dst, dst, send_sem.at[i, c, k], recv_sem.at[i, c, k], lax.rem(me + 2 * k, n))

    def pass_own(i, c):
        src, dst = kinds[i]
        return remote(
            src.at[:, cols(c)], dst.at[rows(me), cols(c)],
            fsend_sem.at[i, c, 0], frecv_sem.at[i, c, 0], partner,
        )

    def pass_on(i, c, k):
        dst = kinds[i][1].at[rows(lax.rem(me + n - 2 * k, n)), cols(c)]
        return remote(dst, dst, fsend_sem.at[i, c, k], frecv_sem.at[i, c, k], partner)

    def passed(i, c, k):
        dst = kinds[i][1].at[rows(lax.rem(partner + n - 2 * k, n)), cols(c)]
        return remote(dst, dst, fsend_sem.at[i, c, k], frecv_sem.at[i, c, k], partner)

    def wsend(k):
        return remote(w_in, w_all.at[me], wsend_sem.at[k], wrecv_sem.at[k], lax.rem(me + 2 * k, n))

    def warrive(k):
        dst = w_all.at[lax.rem(me + n - 2 * k, n)]
        return remote(dst, dst, wsend_sem.at[k], wrecv_sem.at[k], lax.rem(me + 2 * k, n))

    def wpass_own():
        return remote(w_in, w_all.at[me], wfsend_sem.at[0], wfrecv_sem.at[0], partner)

    def wpass_on(k):
        dst = w_all.at[lax.rem(me + n - 2 * k, n)]
        return remote(dst, dst, wfsend_sem.at[k], wfrecv_sem.at[k], partner)

    def wpassed(k):
        dst = w_all.at[lax.rem(partner + n - 2 * k, n)]
        return remote(dst, dst, wfsend_sem.at[k], wfrecv_sem.at[k], partner)

    @pl.loop(0, chunks)
    def _(c):
        for i in range(2):
            pass_own(i, c).start()

        @pl.loop(1, half)
        def _(k):
            for i in range(2):
                send(i, c, k).start()

    wpass_own().start()

    @pl.loop(1, half)
    def _(k):
        wsend(k).start()

    acc[...] = jnp.zeros_like(acc)
    for copy in own:
        copy.wait()

    @pl.loop(0, chunks)
    def _(c):
        @pl.loop(1, half)
        def _(k):
            for i in range(2):
                arrive(i, c, k).wait_recv()
                pass_on(i, c, k).start()

        @pl.loop(0, half)
        def _(k):
            for i in range(2):
                passed(i, c, k).wait_recv()

        @pl.loop(0, experts)
        def _(e):
            for m in range(3):
                slot = e * 3 + m
                tile(c, e, m).wait()
                right = (x_all, x_all, dy_all)[m][:, cols(c)]
                acc[slot] += lax.dot_general(
                    wbuf[slot], right, (((1,), (1,)), ((), ())),
                    preferred_element_type=jnp.float32,
                )

                @pl.when(c + 1 < chunks)
                def _():
                    tile(c + 1, e, m).start()

    @pl.loop(1, half)
    def _(k):
        warrive(k).wait_recv()
        wpass_on(k).start()

    @pl.loop(0, half)
    def _(k):
        wpassed(k).wait_recv()

    weights = jnp.sum(w_all[...], axis=0)
    strip = 32
    sg[...] = jnp.zeros_like(sg)
    for e in range(experts):
        weight = weights[e : e + 1, :]

        def body(r, total):
            part = pl.ds(pl.multiple_of(r * strip, strip), strip)
            gate, up, back = acc[e * 3, part], acc[e * 3 + 1, part], acc[e * 3 + 2, part]
            sig = jax.nn.sigmoid(gate)
            silu = gate * sig
            act = silu * up
            dact = weight * back
            du_t[e, part] = (dact * silu).astype(jnp.bfloat16)
            dg_t[e, part] = (dact * up * sig * (1.0 + gate * (1.0 - sig))).astype(jnp.bfloat16)
            aw_t[e, part] = (act * weight).astype(jnp.bfloat16)
            return total + jnp.sum(act * back, axis=0, keepdims=True)

        sg[e : e + 1, :] = lax.fori_loop(
            0, hidden // strip, body, jnp.zeros((1, tokens), jnp.float32)
        )

    @pl.loop(0, chunks)
    def _(c):
        for i in range(2):
            pass_own(i, c).wait_send()

        @pl.loop(1, half)
        def _(k):
            for i in range(2):
                send(i, c, k).wait_send()
                pass_on(i, c, k).wait_send()

    wpass_own().wait_send()

    @pl.loop(1, half)
    def _(k):
        wsend(k).wait_send()
        wpass_on(k).wait_send()


def grads_kernel(dg_t, du_t, aw_t, x, dy, out_g, out_u, out_d):
    for left, right, out in ((dg_t, x, out_g), (du_t, x, out_u), (aw_t, dy, out_d)):
        out[0] = jnp.dot(left[0], right[...], preferred_element_type=jnp.float32).astype(out.dtype)


def back_kernel(
    n, ne, dgu, sg, w_gate, w_up, out, gate_out,
    wbuf, acc, part, rbuf, csum, gbuf, ebuf, s_r, s_c, s_g,
    wsem, psend, precv, csend, crecv, esend, erecv,
):
    experts, hidden, width = w_gate.shape
    chunks, half = CHUNKS, n // 2
    dc = width // chunks
    tb = out.shape[0]
    me, ep = lax.axis_index("blk"), lax.axis_index("ep")
    core = lax.rem(me, 2)
    chip = me // 2
    partner = me + 1 - 2 * core
    mats = (w_gate, w_up)
    f32, bf16 = jnp.float32, jnp.bfloat16

    def cols(c):
        return pl.ds(pl.multiple_of(c * dc, dc), dc)

    def rows(q):
        return pl.ds(pl.multiple_of(q * tb, tb), tb)

    def tile(c, e, m):
        slot = e * 2 + m
        return pltpu.make_async_copy(mats[m].at[e, :, cols(c)], wbuf.at[slot], wsem.at[slot])

    def remote(src, dst, ssem, rsem, **to):
        return pltpu.make_async_remote_copy(
            src_ref=src, dst_ref=dst, send_sem=ssem, recv_sem=rsem,
            device_id=to, device_id_type=MESH,
        )

    def to_partner(c):
        return remote(part.at[c, 1 - core], rbuf.at[c], psend.at[c], precv.at[c], blk=partner)

    def to_chip(c, k):
        q = lax.rem(chip + k, half)
        return remote(
            csum.at[c, rows(q)], gbuf.at[c, k], csend.at[c, k], crecv.at[c, k], blk=2 * q + core
        )

    def to_ep(c, k):
        return remote(
            ebuf.at[c, ep], ebuf.at[c, ep], esend.at[c, k], erecv.at[c, k], ep=lax.rem(ep + k, ne)
        )

    def from_ep(c, k):
        dst = ebuf.at[c, lax.rem(ep + ne - k, ne)]
        return remote(dst, dst, esend.at[c, k], erecv.at[c, k], ep=lax.rem(ep + k, ne))

    def g_partner():
        return remote(sg, s_r, psend.at[chunks], precv.at[chunks], blk=partner)

    def g_chip(k):
        q = lax.rem(chip + k, half)
        return remote(s_c, s_g.at[k], csend.at[chunks, k], crecv.at[chunks, k], blk=2 * q + core)

    def g_ep(k):
        return remote(
            gate_out.at[ep], gate_out.at[ep], esend.at[chunks, k], erecv.at[chunks, k],
            ep=lax.rem(ep + k, ne),
        )

    def g_from_ep(k):
        dst = gate_out.at[lax.rem(ep + ne - k, ne)]
        return remote(
            dst, dst, esend.at[chunks, k], erecv.at[chunks, k], ep=lax.rem(ep + k, ne)
        )

    for e in range(experts):
        for m in range(2):
            tile(0, e, m).start()
    greet(
        [partner] + [lax.rem(me + 2 * k, n) for k in range(1, half)],
        [lax.rem(ep + k, ne) for k in range(1, ne)],
    )
    g_partner().start()

    @pl.loop(0, chunks + 3)
    def _(step):
        @pl.when(step < chunks)
        def _():
            c = step
            for e in range(experts):
                for m in range(2):
                    slot = e * 2 + m
                    tile(c, e, m).wait()
                    term = jnp.dot(dgu[e, m], wbuf[slot], preferred_element_type=f32)
                    if slot == 0:
                        acc[...] = term
                    else:
                        acc[...] += term

                    @pl.when(c + 1 < chunks)
                    def _():
                        tile(c + 1, e, m).start()

            for q in range(half):
                for p in range(2):
                    part[c, p, q * tb : (q + 1) * tb, :] = acc[
                        (2 * q + p) * tb : (2 * q + p + 1) * tb, :
                    ].astype(bf16)
            to_partner(c).start()

        @pl.when((step >= 1) & (step < chunks + 1))
        def _():
            c = step - 1
            to_partner(c).wait_recv()
            csum[c] = (part[c, core].astype(f32) + rbuf[c].astype(f32)).astype(bf16)

            @pl.loop(1, half)
            def _(k):
                to_chip(c, k).start()

        @pl.when(step == 1)
        def _():
            g_partner().wait_recv()
            s_c[...] = sg[...] + s_r[...]

            @pl.loop(1, half)
            def _(k):
                g_chip(k).start()

        @pl.when((step >= 2) & (step < chunks + 2))
        def _():
            c = step - 2

            @pl.loop(1, half)
            def _(k):
                to_chip(c, k).wait_recv()

            total = csum[c, rows(chip)].astype(f32)
            for k in range(1, half):
                total = total + gbuf[c, k].astype(f32)
            ebuf[c, ep] = total.astype(bf16)

            for k in range(1, ne):
                to_ep(c, k).start()

        @pl.when(step == 2)
        def _():
            @pl.loop(1, half)
            def _(k):
                g_chip(k).wait_recv()

            total = s_c[...]
            for k in range(1, half):
                total = total + s_g[k]
            gate_out[ep] = total
            for k in range(1, ne):
                g_ep(k).start()

        @pl.when(step >= 3)
        def _():
            c = step - 3
            for k in range(1, ne):
                from_ep(c, k).wait_recv()
            total = ebuf[c, 0].astype(f32)
            for k in range(1, ne):
                total = total + ebuf[c, k].astype(f32)
            out[:, cols(c)] = total.astype(bf16)

    for k in range(1, ne):
        g_from_ep(k).wait_recv()
        g_ep(k).wait_send()
    g_partner().wait_send()

    @pl.loop(1, half)
    def _(k):
        g_chip(k).wait_send()

    @pl.loop(0, chunks)
    def _(c):
        to_partner(c).wait_send()
        for k in range(1, ne):
            to_ep(c, k).wait_send()

        @pl.loop(1, half)
        def _(k):
            to_chip(c, k).wait_send()


def shards(n, ne, hidden_in, out_grad, expert_ids, gate_values, w_gate, w_up, w_down):
    tb, width = hidden_in.shape
    experts, hidden, _ = w_gate.shape
    tokens, half, chunks = tb * n, n // 2, CHUNKS
    dc = width // chunks
    me, ep = lax.axis_index("blk"), lax.axis_index("ep")
    f32, bf16 = jnp.float32, jnp.bfloat16
    lines = -(-experts // 8) * 8

    numbers = ep * experts + jnp.arange(lines, dtype=jnp.int32)
    held = (jnp.arange(lines) < experts)[:, None]
    weight = jnp.zeros((lines, tb), f32)
    for k in range(expert_ids.shape[1]):
        hit = (expert_ids[:, k][None, :] == numbers[:, None]) & held
        weight = weight + jnp.where(hit, gate_values[:, k].astype(f32)[None, :], 0.0)
    mine = (jnp.arange(tokens) // tb == me)[None, :]
    weight = jnp.where(mine, jnp.tile(weight, (1, n)), 0.0)

    any_spec = pl.BlockSpec(memory_space=pl.ANY)
    vmem_spec = pl.BlockSpec(memory_space=pltpu.VMEM)
    dma = pltpu.SemaphoreType.DMA
    x_all, dy_all, dg_t, du_t, aw_t, sg = pl.pallas_call(
        functools.partial(forward_kernel, n),
        out_shape=[
            jax.ShapeDtypeStruct((tokens, width), bf16),
            jax.ShapeDtypeStruct((tokens, width), bf16),
            jax.ShapeDtypeStruct((experts, hidden, tokens), bf16),
            jax.ShapeDtypeStruct((experts, hidden, tokens), bf16),
            jax.ShapeDtypeStruct((experts, hidden, tokens), bf16),
            jax.ShapeDtypeStruct((lines, tokens), f32),
        ],
        in_specs=[any_spec] * 6,
        out_specs=[vmem_spec] * 6,
        scratch_shapes=[
            pltpu.VMEM((n, lines, tokens), f32),
            pltpu.VMEM((3 * experts, hidden, dc), bf16),
            pltpu.VMEM((3 * experts, hidden, tokens), f32),
            dma((3 * experts,)),
            dma((3,)),
            dma((2, chunks, half)),
            dma((2, chunks, half)),
            dma((2, chunks, half)),
            dma((2, chunks, half)),
            dma((half,)),
            dma((half,)),
            dma((half,)),
            dma((half,)),
        ],
        compiler_params=pltpu.CompilerParams(
            collective_id=0, has_side_effects=True, vmem_limit_bytes=VMEM_LIMIT
        ),
        name="gather_forward",
    )(hidden_in, out_grad, weight, w_gate, w_up, w_down)

    dgu = jnp.swapaxes(jnp.stack([dg_t, du_t], axis=1), 2, 3)
    input_grad, gate_all = pl.pallas_call(
        functools.partial(back_kernel, n, ne),
        out_shape=[
            jax.ShapeDtypeStruct((tb, width), bf16),
            jax.ShapeDtypeStruct((ne, lines, tokens), f32),
        ],
        in_specs=[vmem_spec, vmem_spec, any_spec, any_spec],
        out_specs=[vmem_spec] * 2,
        scratch_shapes=[
            pltpu.VMEM((2 * experts, hidden, dc), bf16),
            pltpu.VMEM((tokens, dc), f32),
            pltpu.VMEM((chunks, 2, tokens // 2, dc), bf16),
            pltpu.VMEM((chunks, tokens // 2, dc), bf16),
            pltpu.VMEM((chunks, tokens // 2, dc), bf16),
            pltpu.VMEM((chunks, half, tb, dc), bf16),
            pltpu.VMEM((chunks, ne, tb, dc), bf16),
            pltpu.VMEM((lines, tokens), f32),
            pltpu.VMEM((lines, tokens), f32),
            pltpu.VMEM((half, lines, tokens), f32),
            dma((2 * experts,)),
            dma((chunks + 1,)),
            dma((chunks + 1,)),
            dma((chunks + 1, half)),
            dma((chunks + 1, half)),
            dma((chunks + 1, ne)),
            dma((chunks + 1, ne)),
        ],
        compiler_params=pltpu.CompilerParams(
            collective_id=1, has_side_effects=True, vmem_limit_bytes=VMEM_LIMIT
        ),
        name="back_scatter",
    )(dgu, sg, w_gate, w_up)

    wide = min(512, width)
    left = pl.BlockSpec((1, hidden, tokens), lambda e, d: (e, 0, 0))
    right = pl.BlockSpec((tokens, wide), lambda e, d: (0, d))
    result = pl.BlockSpec((1, hidden, wide), lambda e, d: (e, 0, d))
    grads = pl.pallas_call(
        grads_kernel,
        grid=(experts, width // wide),
        out_shape=[jax.ShapeDtypeStruct((experts, hidden, width), bf16)] * 3,
        in_specs=[left] * 3 + [right] * 2,
        out_specs=[result] * 3,
        compiler_params=pltpu.CompilerParams(vmem_limit_bytes=VMEM_LIMIT),
        name="weight_grads",
    )(dg_t, du_t, aw_t, x_all, dy_all)

    by_expert = gate_all[:, :experts].reshape(ne * experts, tokens)
    by_expert = lax.dynamic_slice_in_dim(by_expert, me * tb, tb, axis=1)
    hits = expert_ids[:, :, None] == jnp.arange(ne * experts)[None, None, :]
    gate_grad = jnp.sum(jnp.where(hits, by_expert.T[:, None, :], 0.0), axis=2)
    return (input_grad, gate_grad, *grads)


def solution(mesh):
    tok = P("blk", None)
    wts = P("ep", "blk", None)
    return jax.shard_map(
        functools.partial(shards, mesh.shape["blk"], mesh.shape["ep"]),
        mesh=mesh,
        in_specs=(tok,) * 4 + (wts,) * 3,
        out_specs=(tok,) * 2 + (wts,) * 3,
        check_vma=False,
    )
```

```python
import functools

import jax
import jax.numpy as jnp
from jax import lax
from jax.experimental import pallas as pl
from jax.experimental.pallas import tpu as pltpu
from jax.sharding import PartitionSpec as P

MESH = pl.DeviceIdType.MESH
CHUNKS = 4
BACK_CHUNKS = 8
VMEM_LIMIT = 62 * 1024 * 1024


def greet(blk_peers, ep_peers):
    barrier = pltpu.get_barrier_semaphore()
    for peer in blk_peers:
        pl.semaphore_signal(barrier, inc=1, device_id={"blk": peer}, device_id_type=MESH)
    for peer in ep_peers:
        pl.semaphore_signal(barrier, inc=1, device_id={"ep": peer}, device_id_type=MESH)
    pl.semaphore_wait(barrier, len(blk_peers) + len(ep_peers))


def forward_kernel(
    n, x_in, dy_in, w_in, w_gate, w_up, w_down,
    x_all, dy_all, dg_t, du_t, aw_t, sg,
    w_all, wbuf, turned, acc, wsem, own_sem, zsend, zrecv, xsend, xrecv, csend, crecv,
):
    experts, hidden, width = w_gate.shape
    tb, tokens = x_in.shape[0], x_all.shape[0]
    chunks, lines = CHUNKS, n // 4
    dc = width // chunks
    mats = (w_gate, w_up, w_down)
    me = lax.axis_index("blk")
    partner = me + 1 - 2 * lax.rem(me, 2)
    across = me + 2 - 4 * lax.rem(me // 2, 2)

    def cols(c):
        return pl.ds(pl.multiple_of(c * dc, dc), dc)

    def rows(o):
        return pl.ds(pl.multiple_of(o * tb, tb), tb)

    def tile(c, e, m):
        slot = e * 3 + m
        return pltpu.make_async_copy(mats[m].at[e, :, cols(c)], wbuf.at[slot], wsem.at[slot])

    for e in range(experts):
        for m in range(3):
            tile(0, e, m).start()
    own = [
        pltpu.make_async_copy(x_in, x_all.at[rows(me)], own_sem.at[0]),
        pltpu.make_async_copy(dy_in, dy_all.at[rows(me)], own_sem.at[1]),
        pltpu.make_async_copy(w_in, w_all.at[me], own_sem.at[2]),
    ]
    for copy in own:
        copy.start()

    greet([partner, across] + [lax.rem(me + 4 * k, n) for k in range(1, lines)], [])

    def remote(src, dst, ssem, rsem, to):
        return pltpu.make_async_remote_copy(
            src_ref=src, dst_ref=dst, send_sem=ssem, recv_sem=rsem,
            device_id={"blk": to}, device_id_type=MESH,
        )

    def held(i, c, o):
        if i == 2:
            return w_all.at[o]
        return (x_all, dy_all)[i].at[rows(o), cols(c)]

    def source(i, c):
        if i == 2:
            return w_in
        return (x_in, dy_in)[i].at[:, cols(c)]

    def origin(dev, k):
        return lax.rem(dev + n - 4 * k, n)

    def far(i, c, k):
        return remote(
            source(i, c), held(i, c, me), zsend.at[i, c, k], zrecv.at[i, c, k],
            lax.rem(me + 4 * k, n),
        )

    def far_here(i, c, k):
        dst = held(i, c, origin(me, k))
        return remote(dst, dst, zsend.at[i, c, k], zrecv.at[i, c, k], lax.rem(me + 4 * k, n))

    def over(i, c, k, dev, first=False):
        dst = held(i, c, origin(dev, k))
        return remote(
            source(i, c) if first else dst, dst, xsend.at[i, c, k], xrecv.at[i, c, k], across
        )

    def pair(i, c, k, dev, first=False):
        dst = held(i, c, origin(dev, k))
        return remote(
            source(i, c) if first else dst, dst, csend.at[i, c, k], crecv.at[i, c, k], partner
        )

    def pair_over(i, c, k, dev):
        dst = held(i, c, origin(dev, k))
        return remote(
            dst, dst, csend.at[i, c, lines + k], crecv.at[i, c, lines + k], partner
        )

    def flip(dev):
        return dev + 2 - 4 * lax.rem(dev // 2, 2)

    def first_stage(c, kinds):
        @pl.loop(1, lines)
        def _(k):
            for i in kinds:
                far_here(i, c, k).wait_recv()
                over(i, c, k, me).start()
                pair(i, c, k, me).start()

    def second_stage(c, kinds):
        @pl.loop(0, lines)
        def _(k):
            for i in kinds:
                over(i, c, k, across).wait_recv()
                pair_over(i, c, k, across).start()

    def third_stage(c, kinds):
        @pl.loop(0, lines)
        def _(k):
            for i in kinds:
                pair(i, c, k, partner).wait_recv()
                pair_over(i, c, k, flip(partner)).wait_recv()

    def begin(c, kinds):
        for i in kinds:
            over(i, c, 0, me, True).start()

        @pl.loop(1, lines)
        def _(k):
            for i in kinds:
                far(i, c, k).start()

        for i in kinds:
            pair(i, c, 0, me, True).start()

    def finish(c, kinds):
        for i in kinds:
            over(i, c, 0, me, True).wait_send()
            pair(i, c, 0, me, True).wait_send()
            pair_over(i, c, 0, across).wait_send()

        @pl.loop(1, lines)
        def _(k):
            for i in kinds:
                far(i, c, k).wait_send()
                over(i, c, k, me).wait_send()
                pair(i, c, k, me).wait_send()
                pair_over(i, c, k, across).wait_send()

    @pl.loop(0, chunks)
    def _(c):
        begin(c, (0, 1))

    begin(0, (2,))
    acc[...] = jnp.zeros_like(acc)
    for copy in own:
        copy.wait()
    first_stage(0, (0, 1))
    second_stage(0, (0, 1))

    def products(c, e):
        for m in range(3):
            slot = e * 3 + m
            tile(c, e, m).wait()
            acc[slot] += jnp.dot(
                wbuf[slot], turned[m // 2], preferred_element_type=jnp.float32
            )

            @pl.when(c + 1 < chunks)
            def _():
                tile(c + 1, e, m).start()

    @pl.loop(0, chunks)
    def _(c):
        @pl.when(c + 1 < chunks)
        def _():
            first_stage(c + 1, (0, 1))

        third_stage(c, (0, 1))
        turned[0] = x_all[:, cols(c)].T
        turned[1] = dy_all[:, cols(c)].T

        @pl.loop(0, experts)
        def _(e):
            @pl.when((e == experts - 1) & (c + 1 < chunks))
            def _():
                second_stage(c + 1, (0, 1))

            products(c, e)

    first_stage(0, (2,))
    second_stage(0, (2,))
    third_stage(0, (2,))

    weights = jnp.sum(w_all[...], axis=0)
    strip = 32
    sg[...] = jnp.zeros_like(sg)
    for e in range(experts):
        weight = weights[e : e + 1, :]

        def body(r, total):
            part = pl.ds(pl.multiple_of(r * strip, strip), strip)
            gate, up, back = acc[e * 3, part], acc[e * 3 + 1, part], acc[e * 3 + 2, part]
            sig = jax.nn.sigmoid(gate)
            silu = gate * sig
            act = silu * up
            dact = weight * back
            du_t[e, part] = (dact * silu).astype(jnp.bfloat16)
            dg_t[e, part] = (dact * up * sig * (1.0 + gate * (1.0 - sig))).astype(jnp.bfloat16)
            aw_t[e, part] = (act * weight).astype(jnp.bfloat16)
            return total + jnp.sum(act * back, axis=0, keepdims=True)

        sg[e : e + 1, :] = lax.fori_loop(
            0, hidden // strip, body, jnp.zeros((1, tokens), jnp.float32)
        )

    @pl.loop(0, chunks)
    def _(c):
        finish(c, (0, 1))

    finish(0, (2,))


def grads_kernel(dg_t, du_t, aw_t, x, dy, out_g, out_u, out_d):
    for left, right, out in ((dg_t, x, out_g), (du_t, x, out_u), (aw_t, dy, out_d)):
        out[0] = jnp.dot(left[0], right[...], preferred_element_type=jnp.float32).astype(out.dtype)


def back_kernel(
    n, ne, dgu, sg, w_gate, w_up, out, gate_out,
    wbuf, acc, part, rbuf, csum, xbuf, xsum, gbuf, ebuf, s_r, s_c, s_x, s_cx, s_g,
    wsem, psend, precv, xsend, xrecv, csend, crecv, esend, erecv,
):
    experts, hidden, width = w_gate.shape
    chunks, lines = BACK_CHUNKS, n // 4
    dc = width // chunks
    tb = out.shape[0]
    me, ep = lax.axis_index("blk"), lax.axis_index("ep")
    core = lax.rem(me, 2)
    side = lax.rem(me // 2, 2)
    line = me // 4
    partner = me + 1 - 2 * core
    across = me + 2 - 4 * side
    mats = (w_gate, w_up)
    f32, bf16 = jnp.float32, jnp.bfloat16

    def cols(c):
        return pl.ds(pl.multiple_of(c * dc, dc), dc)

    def rows(q):
        return pl.ds(pl.multiple_of(q * tb, tb), tb)

    def tile(c, e, m):
        slot = e * 2 + m
        return pltpu.make_async_copy(mats[m].at[e, :, cols(c)], wbuf.at[slot], wsem.at[slot])

    def remote(src, dst, ssem, rsem, **to):
        return pltpu.make_async_remote_copy(
            src_ref=src, dst_ref=dst, send_sem=ssem, recv_sem=rsem,
            device_id=to, device_id_type=MESH,
        )

    def to_partner(c):
        return remote(part.at[c, 1 - core], rbuf.at[c], psend.at[c], precv.at[c], blk=partner)

    def to_side(c):
        return remote(csum.at[c, 1 - side], xbuf.at[c], xsend.at[c], xrecv.at[c], blk=across)

    def to_line(c, k):
        q = lax.rem(line + k, lines)
        return remote(
            xsum.at[c, rows(q)], gbuf.at[c, k], csend.at[c, k], crecv.at[c, k],
            blk=4 * q + 2 * side + core,
        )

    def to_ep(c, k):
        return remote(
            ebuf.at[c, ep], ebuf.at[c, ep], esend.at[c, k], erecv.at[c, k], ep=lax.rem(ep + k, ne)
        )

    def from_ep(c, k):
        dst = ebuf.at[c, lax.rem(ep + ne - k, ne)]
        return remote(dst, dst, esend.at[c, k], erecv.at[c, k], ep=lax.rem(ep + k, ne))

    def g_partner():
        return remote(sg, s_r, psend.at[chunks], precv.at[chunks], blk=partner)

    def g_side():
        return remote(s_c, s_x, xsend.at[chunks], xrecv.at[chunks], blk=across)

    def g_line(k):
        q = lax.rem(line + k, lines)
        return remote(
            s_cx, s_g.at[k], csend.at[chunks, k], crecv.at[chunks, k],
            blk=4 * q + 2 * side + core,
        )

    def g_ep(k):
        return remote(
            gate_out.at[ep], gate_out.at[ep], esend.at[chunks, k], erecv.at[chunks, k],
            ep=lax.rem(ep + k, ne),
        )

    def g_from_ep(k):
        dst = gate_out.at[lax.rem(ep + ne - k, ne)]
        return remote(
            dst, dst, esend.at[chunks, k], erecv.at[chunks, k], ep=lax.rem(ep + k, ne)
        )

    for e in range(experts):
        for m in range(2):
            tile(0, e, m).start()
    greet(
        [partner, across] + [lax.rem(me + 4 * k, n) for k in range(1, lines)],
        [lax.rem(ep + k, ne) for k in range(1, ne)],
    )
    g_partner().start()

    @pl.loop(0, chunks + 4)
    def _(step):
        @pl.when(step < chunks)
        def _():
            c = step
            for e in range(experts):
                for m in range(2):
                    slot = e * 2 + m
                    tile(c, e, m).wait()
                    term = jnp.dot(dgu[e, m], wbuf[slot], preferred_element_type=f32)
                    if slot == 0:
                        acc[...] = term
                    else:
                        acc[...] += term

                    @pl.when(c + 1 < chunks)
                    def _():
                        tile(c + 1, e, m).start()

            for q in range(lines):
                for x in range(2):
                    for p in range(2):
                        row = (4 * q + 2 * x + p) * tb
                        part[c, p, x, q * tb : (q + 1) * tb, :] = acc[
                            row : row + tb, :
                        ].astype(bf16)
            to_partner(c).start()

        @pl.when((step >= 1) & (step < chunks + 1))
        def _():
            c = step - 1
            to_partner(c).wait_recv()
            csum[c] = (part[c, core].astype(f32) + rbuf[c].astype(f32)).astype(bf16)
            to_side(c).start()

        @pl.when(step == 1)
        def _():
            g_partner().wait_recv()
            s_c[...] = sg[...] + s_r[...]
            g_side().start()

        @pl.when((step >= 2) & (step < chunks + 2))
        def _():
            c = step - 2
            to_side(c).wait_recv()
            xsum[c] = (csum[c, side].astype(f32) + xbuf[c].astype(f32)).astype(bf16)

            @pl.loop(1, lines)
            def _(k):
                to_line(c, k).start()

        @pl.when(step == 2)
        def _():
            g_side().wait_recv()
            s_cx[...] = s_c[...] + s_x[...]

            @pl.loop(1, lines)
            def _(k):
                g_line(k).start()

        @pl.when((step >= 3) & (step < chunks + 3))
        def _():
            c = step - 3

            @pl.loop(1, lines)
            def _(k):
                to_line(c, k).wait_recv()

            total = xsum[c, rows(line)].astype(f32)
            for k in range(1, lines):
                total = total + gbuf[c, k].astype(f32)
            ebuf[c, ep] = total.astype(bf16)

            for k in range(1, ne):
                to_ep(c, k).start()

        @pl.when(step == 3)
        def _():
            @pl.loop(1, lines)
            def _(k):
                g_line(k).wait_recv()

            total = s_cx[...]
            for k in range(1, lines):
                total = total + s_g[k]
            gate_out[ep] = total
            for k in range(1, ne):
                g_ep(k).start()

        @pl.when(step >= 4)
        def _():
            c = step - 4
            for k in range(1, ne):
                from_ep(c, k).wait_recv()
            total = ebuf[c, 0].astype(f32)
            for k in range(1, ne):
                total = total + ebuf[c, k].astype(f32)
            out[:, cols(c)] = total.astype(bf16)

    for k in range(1, ne):
        g_from_ep(k).wait_recv()
        g_ep(k).wait_send()
    g_partner().wait_send()

    g_side().wait_send()

    @pl.loop(1, lines)
    def _(k):
        g_line(k).wait_send()

    @pl.loop(0, chunks)
    def _(c):
        to_partner(c).wait_send()
        to_side(c).wait_send()
        for k in range(1, ne):
            to_ep(c, k).wait_send()

        @pl.loop(1, lines)
        def _(k):
            to_line(c, k).wait_send()


def shards(n, ne, hidden_in, out_grad, expert_ids, gate_values, w_gate, w_up, w_down):
    tb, width = hidden_in.shape
    experts, hidden, _ = w_gate.shape
    tokens, half, chunks = tb * n, n // 2, CHUNKS
    dc = width // chunks
    back, bdc = BACK_CHUNKS, width // BACK_CHUNKS
    me, ep = lax.axis_index("blk"), lax.axis_index("ep")
    f32, bf16 = jnp.float32, jnp.bfloat16
    lines = -(-experts // 8) * 8

    numbers = ep * experts + jnp.arange(lines, dtype=jnp.int32)
    held = (jnp.arange(lines) < experts)[:, None]
    weight = jnp.zeros((lines, tb), f32)
    for k in range(expert_ids.shape[1]):
        hit = (expert_ids[:, k][None, :] == numbers[:, None]) & held
        weight = weight + jnp.where(hit, gate_values[:, k].astype(f32)[None, :], 0.0)
    mine = (jnp.arange(tokens) // tb == me)[None, :]
    weight = jnp.where(mine, jnp.tile(weight, (1, n)), 0.0)

    any_spec = pl.BlockSpec(memory_space=pl.ANY)
    vmem_spec = pl.BlockSpec(memory_space=pltpu.VMEM)
    dma = pltpu.SemaphoreType.DMA
    x_all, dy_all, dg_t, du_t, aw_t, sg = pl.pallas_call(
        functools.partial(forward_kernel, n),
        out_shape=[
            jax.ShapeDtypeStruct((tokens, width), bf16),
            jax.ShapeDtypeStruct((tokens, width), bf16),
            jax.ShapeDtypeStruct((experts, hidden, tokens), bf16),
            jax.ShapeDtypeStruct((experts, hidden, tokens), bf16),
            jax.ShapeDtypeStruct((experts, hidden, tokens), bf16),
            jax.ShapeDtypeStruct((lines, tokens), f32),
        ],
        in_specs=[any_spec] * 6,
        out_specs=[vmem_spec] * 6,
        scratch_shapes=[
            pltpu.VMEM((n, lines, tokens), f32),
            pltpu.VMEM((3 * experts, hidden, dc), bf16),
            pltpu.VMEM((2, dc, tokens), bf16),
            pltpu.VMEM((3 * experts, hidden, tokens), f32),
            dma((3 * experts,)),
            dma((3,)),
            dma((3, chunks, half // 2)),
            dma((3, chunks, half // 2)),
            dma((3, chunks, half // 2)),
            dma((3, chunks, half // 2)),
            dma((3, chunks, half)),
            dma((3, chunks, half)),
        ],
        compiler_params=pltpu.CompilerParams(
            collective_id=0, has_side_effects=True, vmem_limit_bytes=VMEM_LIMIT
        ),
        name="gather_forward",
    )(hidden_in, out_grad, weight, w_gate, w_up, w_down)

    dgu = jnp.swapaxes(jnp.stack([dg_t, du_t], axis=1), 2, 3)
    input_grad, gate_all = pl.pallas_call(
        functools.partial(back_kernel, n, ne),
        out_shape=[
            jax.ShapeDtypeStruct((tb, width), bf16),
            jax.ShapeDtypeStruct((ne, lines, tokens), f32),
        ],
        in_specs=[vmem_spec, vmem_spec, any_spec, any_spec],
        out_specs=[vmem_spec] * 2,
        scratch_shapes=[
            pltpu.VMEM((2 * experts, hidden, bdc), bf16),
            pltpu.VMEM((tokens, bdc), f32),
            pltpu.VMEM((back, 2, 2, tokens // 4, bdc), bf16),
            pltpu.VMEM((back, 2, tokens // 4, bdc), bf16),
            pltpu.VMEM((back, 2, tokens // 4, bdc), bf16),
            pltpu.VMEM((back, tokens // 4, bdc), bf16),
            pltpu.VMEM((back, tokens // 4, bdc), bf16),
            pltpu.VMEM((back, n // 4, tb, bdc), bf16),
            pltpu.VMEM((back, ne, tb, bdc), bf16),
            pltpu.VMEM((lines, tokens), f32),
            pltpu.VMEM((lines, tokens), f32),
            pltpu.VMEM((lines, tokens), f32),
            pltpu.VMEM((lines, tokens), f32),
            pltpu.VMEM((n // 4, lines, tokens), f32),
            dma((2 * experts,)),
            dma((back + 1,)),
            dma((back + 1,)),
            dma((back + 1,)),
            dma((back + 1,)),
            dma((back + 1, n // 4)),
            dma((back + 1, n // 4)),
            dma((back + 1, ne)),
            dma((back + 1, ne)),
        ],
        compiler_params=pltpu.CompilerParams(
            collective_id=1, has_side_effects=True, vmem_limit_bytes=VMEM_LIMIT
        ),
        name="back_scatter",
    )(dgu, sg, w_gate, w_up)

    wide = min(512, width)
    left = pl.BlockSpec((1, hidden, tokens), lambda e, d: (e, 0, 0))
    right = pl.BlockSpec((tokens, wide), lambda e, d: (0, d))
    result = pl.BlockSpec((1, hidden, wide), lambda e, d: (e, 0, d))
    grads = pl.pallas_call(
        grads_kernel,
        grid=(experts, width // wide),
        out_shape=[jax.ShapeDtypeStruct((experts, hidden, width), bf16)] * 3,
        in_specs=[left] * 3 + [right] * 2,
        out_specs=[result] * 3,
        compiler_params=pltpu.CompilerParams(vmem_limit_bytes=VMEM_LIMIT),
        name="weight_grads",
    )(dg_t, du_t, aw_t, x_all, dy_all)

    by_expert = gate_all[:, :experts].reshape(ne * experts, tokens)
    by_expert = lax.dynamic_slice_in_dim(by_expert, me * tb, tb, axis=1)
    hits = expert_ids[:, :, None] == jnp.arange(ne * experts)[None, None, :]
    gate_grad = jnp.sum(jnp.where(hits, by_expert.T[:, None, :], 0.0), axis=2)
    return (input_grad, gate_grad, *grads)


def solution(mesh):
    tok = P("blk", None)
    wts = P("ep", "blk", None)
    return jax.shard_map(
        functools.partial(shards, mesh.shape["blk"], mesh.shape["ep"]),
        mesh=mesh,
        in_specs=(tok,) * 4 + (wts,) * 3,
        out_specs=(tok,) * 2 + (wts,) * 3,
        check_vma=False,
    )
```
